256 devices in a mesh: row: 16 (over x, z_hi, core), col: 16 (over z_lo, y).
Axes of the slice: x: 4, y: 4, z: 8 (z_hi: 2, z_lo: 4; z = z_hi * 4 + z_lo), core: 2. Of those that a mesh axis runs over, the one named last changes fastest.
Arguments:
- diag_coords: int32 [2, 1536], replicated, may hold values from 0 to 32767
- panel_coords: int32 [2, 16, 1536], P(None, 'row', 'col'), may hold values from 0 to 32767
- test_matrix: bfloat16 [16, 1536, 512], P('row', 'col'), may hold values from -6 to 6
- ranks: int32 [16], replicated, may hold values from 64 to 512, as said below
Outputs:
- panel_left: bfloat16 [16, 1536, 512], P('row', 'col')
- update_right: bfloat16 [16, 16, 1536, 512], P('row', 'col')
The draws below stay inside these ranges and needn't reach their ends.
Inputs may be any that keep to these rules, and one draw needn't show every extreme that they name: ranks[i] is 512 at tile 0 and 64 at the last tile and falls roughly evenly in between, with small random steps.
All inputs are finite; a program needn't handle non-finite values.
Results may differ from the reference program's by a relative error of at most 0.0068.
Values may be sent and summed in bfloat16 or wider, within the bound.
No kernel may reach another device: no remote copies, remote signals or barrier semaphores. Data moves between devices by JAX's collectives and lax.ppermute only.
A program may use at most 192 MiB of HBM per device.

```python
import jax
import jax.numpy as jnp
from jax import lax

NB = 1536
R = 512
MT = 16


def draw_ranks(key, part):
    index = jnp.arange(MT, dtype=jnp.int32)
    base = R - (R - R // 8) * index // (MT - 1)
    jitter = jax.random.randint(key, (MT,), 0, R // 16 + 1)
    inner = ((index > 0) & (index < MT - 1)).astype(jnp.int32)
    values = jnp.maximum(base - jitter * inner, R // 8)
    return values.astype(jnp.int32)


def place_ends(entries, stream_key, least, top_value):
    extent = entries.shape
    place = [jax.random.randint(jax.random.fold_in(stream_key, axis), (), 0, extent[axis]) for axis in range(len(extent))]
    entries = entries.at[tuple(place)].set(least)
    longest = extent.index(max(extent))
    place[longest] = (place[longest] + 1) % extent[longest]
    return entries.at[tuple(place)].set(top_value)


def steps_of(own_key, shape, split, low, high):
    loudness, own = 1.0, jax.random.fold_in(own_key, 6)
    for axis_at, blocks in split:
        draws = jnp.exp(jax.random.uniform(jax.random.fold_in(own, axis_at), (blocks,), jnp.float32, low / len(split), high / len(split)))
        loudness = loudness * jnp.repeat(draws, shape[axis_at] // blocks).reshape([-1 if axis == axis_at else 1 for axis in range(len(shape))])
    return loudness


def noise(stream_key, extent, width, most, pieces=(), held_as=jnp.bfloat16):
    loudness = steps_of(stream_key, extent, pieces, -0.22, 0.18) if pieces else 1.0
    array = jax.random.normal(stream_key, extent, jnp.float32) * width * loudness
    return jnp.minimum(jnp.maximum(array, -most), most).astype(held_as)


def setup_inputs(seed: int = 0) -> dict:
    key_of = jax.random.split(jax.random.key(seed), 5)
    diag_coords = place_ends(jax.random.randint(key_of[0], (2, NB), 0, 32768), jax.random.fold_in(key_of[0], 1), 0, 32767).astype(jnp.int32)
    panel_coords = place_ends(jax.random.randint(key_of[1], (2, MT, NB), 0, 32768), jax.random.fold_in(key_of[1], 1), 0, 32767).astype(jnp.int32)
    test_matrix = noise(key_of[2], (MT, NB, R), 1.0, 6.0, ((0, 16), (1, 16)))
    ranks = draw_ranks(jax.random.fold_in(key_of[4], 71), 0)
    return {"diag_coords": diag_coords, "panel_coords": panel_coords, "test_matrix": test_matrix, "ranks": ranks}


range_length = 409.6
nugget = 0.5
shift_ratio = 0.01

def matern(first, second):
    delta_x = (first[0][:, None] - second[0][None, :]).astype(jnp.float32)
    delta_y = (first[1][:, None] - second[1][None, :]).astype(jnp.float32)
    return jnp.exp(-jnp.sqrt(delta_x * delta_x + delta_y * delta_y) / range_length)

def reference(diag_coords, panel_coords, test_matrix, ranks):
    cov = matern(diag_coords, diag_coords) + nugget * jnp.eye(NB, dtype=jnp.float32)
    lower = jnp.linalg.cholesky(cov)
    columns = jnp.arange(R, dtype=jnp.int32)
    masks = (columns[None, :] < ranks[:, None]).astype(jnp.bfloat16)
    tests = test_matrix * masks[:, None, :]

    def panel_tile(inputs):
        points, test, mask, rank = inputs
        block = matern(points, diag_coords)
        solved = jax.scipy.linalg.solve_triangular(lower, block.T, lower=True).T
        sample = jnp.dot(solved, test.astype(jnp.float32), precision=lax.Precision.HIGHEST)
        gram = jnp.dot(sample.T, sample, precision=lax.Precision.HIGHEST)
        maskf = mask.astype(jnp.float32)
        shift = shift_ratio * jnp.sum(jnp.diagonal(gram)) / rank.astype(jnp.float32)
        shifted = gram + jnp.diag(shift * maskf + 1.0 - maskf)
        factor = jnp.linalg.cholesky(shifted)
        basis = jax.scipy.linalg.solve_triangular(factor, sample.T, lower=True).T
        basis = basis.astype(jnp.bfloat16)
        coeff = jnp.dot(solved.T, basis.astype(jnp.float32), precision=lax.Precision.HIGHEST)
        return (basis, coeff.astype(jnp.bfloat16))
    left, coeff = lax.map(panel_tile, (jnp.transpose(panel_coords, (1, 0, 2)), tests, masks, ranks))

    def update_row(coeff_row):
        core = jnp.einsum('nr,jns->jrs', coeff_row.astype(jnp.float32), coeff.astype(jnp.float32))
        core = core.astype(jnp.bfloat16)
        return jnp.einsum('jns,jrs->jnr', left.astype(jnp.float32), core.astype(jnp.float32)).astype(jnp.bfloat16)
    update = lax.map(update_row, coeff)
    return (left, update)
```

```python
import jax
import jax.numpy as jnp
from jax import lax
from jax.experimental import pallas as pl
from jax.experimental.pallas import tpu as pltpu
from jax.sharding import PartitionSpec as P

range_length = 409.6
nugget = 0.5
shift_ratio = 0.01

F32 = jnp.float32
BF = jnp.bfloat16


def split2(a):
    hi = a.astype(BF)
    lo = (a - hi.astype(F32)).astype(BF)
    return hi, lo


def split3(a):
    hi = a.astype(BF)
    r = a - hi.astype(F32)
    mid = r.astype(BF)
    return hi, mid, (r - mid.astype(F32)).astype(BF)


def dot_nn(a, b):
    return lax.dot_general(a, b, (((1,), (0,)), ((), ())), preferred_element_type=F32)


def dot_nt(a, b):
    return lax.dot_general(a, b, (((1,), (1,)), ((), ())), preferred_element_type=F32)


def mul_pieces(a, b, dot, axis_b):
    if len(a) == 2:
        ah, al = a
        bh, bl = b
        return dot(jnp.concatenate([ah, al], 1), jnp.concatenate([bh, bh], axis_b)) + dot(ah, bl)
    ah, am, al = a
    bh, bm, bl = b
    hm = jnp.concatenate([ah, am], 1)
    out = dot(jnp.concatenate([ah, al], 1), jnp.concatenate([bl, bh], axis_b))
    out = out + dot(hm, jnp.concatenate([bm, bm], axis_b))
    return out + dot(hm, jnp.concatenate([bh, bh], axis_b))


def factor_block(mats):
    sub = lax.broadcasted_iota(jnp.int32, (8, 128), 0)
    lane = lax.broadcasted_iota(jnp.int32, (8, 128), 1)

    def sb(a, p):
        return jnp.broadcast_to(a[p:p + 1, :], (8, 128))

    def lb(a, c):
        return jnp.broadcast_to(a[:, c:c + 1], (8, 128))

    nb = len(mats)
    S = [list(m) for m in mats]
    I = [[jnp.where(lane == sub + 8 * v, 1.0, 0.0).astype(F32) for v in range(16)] for _ in mats]
    out = [[None] * 16 for _ in mats]
    for g in range(16):
        st = []
        for b in range(nb):
            U, E = S[b][g], I[b][g]
            C = [lb(U, 8 * g + t) for t in range(8)]
            st.append([U, E, C, [], []])
        for p in range(8):
            for b in range(nb):
                U, E, C, rinvs, ust = st[b]
                rinv = 1.0 / sb(C[p], p)
                rows = {t: sb(C[t], p) for t in range(p + 1, 8)}
                m = jnp.where(sub > p, C[p] * rinv, 0.0)
                for t in range(p + 1, 8):
                    C[t] = C[t] - m * rows[t]
                st[b][0] = U - m * sb(U, p)
                st[b][1] = E - m * sb(E, p)
                rinvs.append(rinv)
                ust.append(rows)
        for b in range(nb):
            U, E, C, rinvs, ust = st[b]
            dv = C[0]
            for p in range(1, 8):
                dv = jnp.where(sub == p, C[p], dv)
            r = lax.rsqrt(dv)
            r = r * (1.5 - 0.5 * dv * r * r)
            out[b][g] = E * r
            Ub = [sb(U, t) for t in range(8)]
            Eb = [sb(E, t) for t in range(8)]
            for v in range(g + 1, 16):
                xs = [lb(S[b][v], 8 * g + t) for t in range(8)]
                ms = []
                for t in range(8):
                    x = xs[t]
                    for s in range(t):
                        x = x - ms[s] * ust[s][t]
                    ms.append(x * rinvs[t])
                sv, iv = S[b][v], I[b][v]
                for t in range(8):
                    sv = sv - ms[t] * Ub[t]
                    iv = iv - ms[t] * Eb[t]
                S[b][v], I[b][v] = sv, iv
    return out


def chol_inv_steps(s_refs, x_refs, n, split, m_ref):
    ch = 512
    nc = n // ch
    nb = len(s_refs)

    def step(k, _):
        o = pl.multiple_of(k * 128, 128)
        mats = [[s[pl.ds(pl.multiple_of(o + 8 * v, 8), 8), pl.ds(o, 128)] for v in range(16)] for s in s_refs]
        ms = factor_block(mats)
        for b in range(nb):
            s, x = s_refs[b], x_refs[b]
            for v in range(16):
                m_ref[b, 8 * v:8 * v + 8, :] = ms[b][v]
            M = split(m_ref[b])
            xk = mul_pieces(M, split(x[pl.ds(o, 128), :]), dot_nn, 0)
            x[pl.ds(o, 128), :] = xk
            xp = split(xk)
            for r in range(nc):
                @pl.when(k + 1 < 4 * (r + 1))
                def _():
                    rid = lax.broadcasted_iota(jnp.int32, (ch, 128), 0) + r * ch
                    def lp_of(c):
                        p = s[c * ch:(c + 1) * ch, pl.ds(o, 128)]
                        lp = mul_pieces(split(p), M, dot_nt, 1)
                        ids = lax.broadcasted_iota(jnp.int32, (ch, 128), 0) + c * ch
                        return split(jnp.where(ids >= o + 128, lp, 0.0))
                    lps = {}
                    lpr = lp_of(r)
                    for c in range(r + 1):
                        @pl.when(k + 1 < 4 * (c + 1))
                        def _():
                            lpc = lpr if c == r else lp_of(c)
                            s[r * ch:(r + 1) * ch, c * ch:(c + 1) * ch] -= mul_pieces(lpr, lpc, dot_nt, 1)

                        @pl.when(k >= 4 * c)
                        def _():
                            cx = tuple(q[:, c * ch:(c + 1) * ch] for q in xp)
                            x[r * ch:(r + 1) * ch, c * ch:(c + 1) * ch] -= mul_pieces(lpr, cx, dot_nn, 0)
        return 0

    lax.fori_loop(0, n // 128, step, 0)


def matern_block(r, c):
    dx = r[:, 0:1] - c[0:1, :]
    dy = r[:, 1:2] - c[1:2, :]
    return jnp.exp(-jnp.sqrt(dx * dx + dy * dy) / range_length)


def cov_kernel(pr_ref, pc_ref, hi_ref, lo_ref, s_ref, x_ref, m_ref):
    n = s_ref.shape[0]
    c = pc_ref[...]

    def build(k, _):
        o = pl.multiple_of(k * 128, 128)
        rows = lax.broadcasted_iota(jnp.int32, (128, n), 0) + o
        cols = lax.broadcasted_iota(jnp.int32, (128, n), 1)
        eye = jnp.where(rows == cols, 1.0, 0.0)
        s_ref[pl.ds(o, 128), :] = matern_block(pr_ref[pl.ds(o, 128), :], c) + nugget * eye
        x_ref[pl.ds(o, 128), :] = eye
        return 0

    lax.fori_loop(0, n // 128, build, 0)
    chol_inv_steps([s_ref], [x_ref], n, split2, m_ref)

    def emit(k, _):
        o = pl.multiple_of(k * 128, 128)
        hi, lo = split2(x_ref[pl.ds(o, 128), :])
        hi_ref[pl.ds(o, 128), :] = hi
        lo_ref[pl.ds(o, 128), :] = lo
        return 0

    lax.fori_loop(0, n // 128, emit, 0)


def cov_factor_inverse(coords):
    n = coords.shape[1]
    xy = coords.astype(F32)
    pc = jnp.concatenate([xy, jnp.zeros((6, n), F32)], 0)
    pr = pc.T
    return pl.pallas_call(
        cov_kernel,
        out_shape=(jax.ShapeDtypeStruct((n, n), BF),) * 2,
        scratch_shapes=[pltpu.VMEM((n, n), F32), pltpu.VMEM((n, n), F32), pltpu.VMEM((1, 128, 128), F32)],
        compiler_params=pltpu.CompilerParams(vmem_limit_bytes=56 << 20),
        name="cov_factor",
    )(pr, pc)


def tile_kernel(
    info_ref, hi_ref, lo_ref, gi_ref, gj_ref, pc_ref, left_ref, upd_ref,
    v_ref, xy_ref, vt_ref, wh_ref, wl_ref, bh_ref, bl_ref, smp_ref, s_ref, x_ref, m_ref, pl_ref, cf_ref,
):
    n = hi_ref.shape[0]
    r = upd_ref.shape[1]
    pieces, local = gi_ref.shape[0], left_ref.shape[0]
    blocks = r // 128
    ch, half = 512, 256
    pc = pc_ref[...]
    cols = lax.broadcasted_iota(jnp.int32, (1, r), 1)
    grow = lax.broadcasted_iota(jnp.int32, (r, r), 0)
    gcol = lax.broadcasted_iota(jnp.int32, (r, r), 1)
    for b in range(2):
        g_ref = (gi_ref, gj_ref)[b]
        rank = info_ref[b]
        mask = cols < rank

        def place(c, _):
            o = pl.multiple_of(c * local, 32)
            for q in range(blocks):
                v_ref[pl.ds(o, local), q * 128:(q + 1) * 128] = g_ref[c, q * local:(q + 1) * local, :]
            d = g_ref[c, blocks * local:blocks * local + 16, :].astype(F32)
            xy_ref[pl.ds(o, local), 0:16] = d.T[0:local, :]
            return 0

        lax.fori_loop(0, pieces, place, 0)

        def turn(k, _):
            o = pl.multiple_of(k * half, half)
            v = jnp.where(mask, v_ref[pl.ds(o, half), :].astype(F32), 0.0)
            vt_ref[:, pl.ds(o, half)] = v.T.astype(BF)
            return 0

        lax.fori_loop(0, n // half, turn, 0)
        for q in range(n // ch):
            o = q * ch
            for h in range(r // half):
                vt = vt_ref[h * half:(h + 1) * half, o:]
                w = dot_nn(vt, hi_ref[o:, o:o + ch]) + dot_nn(vt, lo_ref[o:, o:o + ch])
                w_hi, w_lo = split2(w)
                wh_ref[h * half:(h + 1) * half, o:o + ch] = w_hi
                wl_ref[h * half:(h + 1) * half, o:o + ch] = w_lo
        s_ref[b] = jnp.zeros((r, r), F32)
        x_ref[b] = jnp.zeros((r, r), F32)

        def draw(k, _):
            o = pl.multiple_of(k * half, half)
            xy = xy_ref[pl.ds(o, half), :]
            x = xy[:, 0:1] * 256.0 + xy[:, 1:2]
            y = xy[:, 2:3] * 256.0 + xy[:, 3:4]
            dx = x - pc[0:1, :]
            dy = y - pc[1:2, :]
            b_hi, b_lo = split2(jnp.exp(-jnp.sqrt(dx * dx + dy * dy) / range_length))
            bh_ref[b, pl.ds(o, half), :] = b_hi
            bl_ref[b, pl.ds(o, half), :] = b_lo
            wh = wh_ref[...]
            smp = dot_nt(b_hi, wl_ref[...]) + dot_nt(b_lo, wh) + dot_nt(b_hi, wh)
            smp_ref[b, pl.ds(o, half), :] = smp
            p_h, p_m, p_l = split3(smp)
            t_h = p_h.astype(F32).T.astype(BF)
            t_m = p_m.astype(F32).T.astype(BF)
            s_ref[b] += dot_nn(t_h, p_h) + dot_nn(t_m, p_m)
            x_ref[b] += dot_nn(t_h, p_m) + dot_nn(t_h, p_l)
            return 0

        lax.fori_loop(0, n // half, draw, 0)
        cross = x_ref[b]
        gram = s_ref[b] + (cross + cross.T)
        eye = grow == gcol
        trace = jnp.sum(jnp.where(eye, gram, 0.0))
        shift = shift_ratio * trace / rank.astype(F32)
        s_ref[b] = gram + jnp.where(eye, jnp.where(gcol < rank, shift, 1.0), 0.0)
        x_ref[b] = jnp.where(eye, 1.0, 0.0)

    chol_inv_steps([s_ref.at[0], s_ref.at[1]], [x_ref.at[0], x_ref.at[1]], r, split3, m_ref)

    for b in range(2):
        inv = split3(x_ref[b])

        def base(k, _):
            o = pl.multiple_of(k * half, half)
            part = mul_pieces(split3(smp_ref[b, pl.ds(o, half), :]), inv, dot_nt, 1).astype(BF)
            pl_ref[b, pl.ds(o, half), :] = part
            vt_ref[:, pl.ds(o, half)] = part.astype(F32).T.astype(BF)
            return 0

        lax.fori_loop(0, n // half, base, 0)
        for q in range(n // ch):
            o = q * ch
            for h in range(r // half):
                lt = vt_ref[h * half:(h + 1) * half, :]
                p = dot_nn(lt, bh_ref[b, :, o:o + ch]) + dot_nn(lt, bl_ref[b, :, o:o + ch])
                p_hi, p_lo = split2(p)
                wh_ref[h * half:(h + 1) * half, o:o + ch] = p_hi
                wl_ref[h * half:(h + 1) * half, o:o + ch] = p_lo
        for q in range(n // half):
            o, e = q * half, (q + 1) * half
            ih = hi_ref[o:e, :e]
            ph = wh_ref[:, :e]
            c = dot_nt(ih, wl_ref[:, :e]) + dot_nt(lo_ref[o:e, :e], ph) + dot_nt(ih, ph)
            cf_ref[b, o:e, :] = c.astype(BF)

    left_ref[...] = pl_ref[0, pl.ds(pl.multiple_of(info_ref[3] * local, 32), local), :]
    core = jnp.zeros((r, r), F32)
    for q in range(n // ch):
        ct = cf_ref[0, q * ch:(q + 1) * ch, :].astype(F32).T.astype(BF)
        core = core + dot_nn(ct, cf_ref[1, q * ch:(q + 1) * ch, :])
    core = core.astype(BF)
    for q in range(n // ch):
        upd_ref[q * ch:(q + 1) * ch, :] = dot_nt(pl_ref[1, q * ch:(q + 1) * ch, :], core).astype(BF)


def tiles(info, inv_hi, inv_lo, own, turned, coords):
    n = inv_hi.shape[0]
    local = n // own.shape[0]
    r = (own.shape[1] - 16) // local * 128
    pc = jnp.concatenate([coords.astype(F32), jnp.zeros((6, n), F32)], 0)
    vmem = pl.BlockSpec(memory_space=pltpu.VMEM)
    return pl.pallas_call(
        tile_kernel,
        in_specs=[pl.BlockSpec(memory_space=pltpu.SMEM)] + [vmem] * 5,
        out_specs=(vmem, vmem),
        out_shape=(jax.ShapeDtypeStruct((local, r), BF), jax.ShapeDtypeStruct((n, r), BF)),
        scratch_shapes=[
            pltpu.VMEM((n, r), BF),
            pltpu.VMEM((n, 128), F32),
            pltpu.VMEM((r, n), BF),
            pltpu.VMEM((r, n), BF),
            pltpu.VMEM((r, n), BF),
            pltpu.VMEM((2, n, n), BF),
            pltpu.VMEM((2, n, n), BF),
            pltpu.VMEM((2, n, r), F32),
            pltpu.VMEM((2, r, r), F32),
            pltpu.VMEM((2, r, r), F32),
            pltpu.VMEM((2, 128, 128), F32),
            pltpu.VMEM((2, n, r), BF),
            pltpu.VMEM((2, n, r), BF),
        ],
        compiler_params=pltpu.CompilerParams(vmem_limit_bytes=63 << 20),
        name="tiles",
    )(info, inv_hi, inv_lo, own, turned, pc)


def shards(diag_coords, panel_coords, test_matrix, ranks):
    n_row = lax.axis_size("row")
    n_col = lax.axis_size("col")
    row_index = lax.axis_index("row")
    col_index = lax.axis_index("col")
    local = panel_coords.shape[2]
    blocks = test_matrix.shape[2] // 128
    digits = jnp.stack([panel_coords[:, 0] >> 8, panel_coords[:, 0] & 255], 1).reshape(4, local).astype(BF)
    digits = jnp.pad(digits, ((0, 12), (0, 128 - local)))
    parts = [test_matrix[0, :, q * 128:(q + 1) * 128] for q in range(blocks)]
    piece = jnp.concatenate(parts + [digits], 0)[None]
    swap = [(r * n_col + c, c * n_col + r) for r in range(n_row) for c in range(n_col)]
    own = lax.all_gather(piece, "col", axis=0, tiled=True)
    turned = lax.all_gather(lax.ppermute(piece, ("row", "col"), swap), "row", axis=0, tiled=True)
    info = jnp.stack([ranks[row_index], ranks[col_index], row_index, col_index]).astype(jnp.int32)
    inv_hi, inv_lo = cov_factor_inverse(diag_coords)
    left, update = tiles(info, inv_hi, inv_lo, own, turned, diag_coords)
    return (left[None], update[None, None])


def solution(mesh):
    in_specs = (P(), P(None, "row", "col"), P("row", "col", None), P())
    out_specs = (P("row", "col", None), P("row", "col", None, None))
    return jax.shard_map(shards, mesh=mesh, in_specs=in_specs, out_specs=out_specs, check_vma=False)
```

```python
import functools
import math

import jax
import jax.numpy as jnp
from jax import lax
from jax.experimental import pallas as pl
from jax.experimental.pallas import tpu as pltpu
from jax.sharding import PartitionSpec as P

F32 = jnp.float32
BF = jnp.bfloat16


def split2(a):
    hi = a.astype(BF)
    lo = (a - hi.astype(F32)).astype(BF)
    return hi, lo


def split3(a):
    hi = a.astype(BF)
    r = a - hi.astype(F32)
    mid = r.astype(BF)
    return hi, mid, (r - mid.astype(F32)).astype(BF)


def dot_nn(a, b):
    return lax.dot_general(a, b, (((1,), (0,)), ((), ())), preferred_element_type=F32)


def dot_nt(a, b):
    return lax.dot_general(a, b, (((1,), (1,)), ((), ())), preferred_element_type=F32)


def mul_pieces(a, b, dot, axis_b):
    if len(a) == 2:
        ah, al = a
        bh, bl = b
        return dot(jnp.concatenate([ah, al], 1), jnp.concatenate([bh, bh], axis_b)) + dot(ah, bl)
    ah, am, al = a
    bh, bm, bl = b
    hm = jnp.concatenate([ah, am], 1)
    out = dot(jnp.concatenate([ah, al], 1), jnp.concatenate([bl, bh], axis_b))
    out = out + dot(hm, jnp.concatenate([bm, bm], axis_b))
    return out + dot(hm, jnp.concatenate([bh, bh], axis_b))


def factor_block(mats, filler=None):
    sub = lax.broadcasted_iota(jnp.int32, (8, 128), 0)
    lane = lax.broadcasted_iota(jnp.int32, (8, 128), 1)

    def sb(a, p):
        return jnp.broadcast_to(a[p:p + 1, :], (8, 128))

    def lb(a, c):
        return jnp.broadcast_to(a[:, c:c + 1], (8, 128))

    nb = len(mats)
    S = [list(m) for m in mats]
    I = [[jnp.where(lane == sub + 8 * v, 1.0, 0.0).astype(F32) for v in range(16)] for _ in mats]
    out = [[None] * 16 for _ in mats]
    for g in range(16):
        if filler is not None:
            filler(g)
        st = []
        for b in range(nb):
            U, E = S[b][g], I[b][g]
            C = [lb(U, 8 * g + t) for t in range(8)]
            st.append([U, E, C, [], []])
        for p in range(8):
            for b in range(nb):
                U, E, C, rinvs, ust = st[b]
                rinv = 1.0 / sb(C[p], p)
                rows = {t: sb(C[t], p) for t in range(p + 1, 8)}
                m = jnp.where(sub > p, C[p] * rinv, 0.0)
                for t in range(p + 1, 8):
                    C[t] = C[t] - m * rows[t]
                st[b][0] = U - m * sb(U, p)
                st[b][1] = E - m * sb(E, p)
                rinvs.append(rinv)
                ust.append(rows)
        for b in range(nb):
            U, E, C, rinvs, ust = st[b]
            dv = C[0]
            for p in range(1, 8):
                dv = jnp.where(sub == p, C[p], dv)
            r = lax.rsqrt(dv)
            r = r * (1.5 - 0.5 * dv * r * r)
            out[b][g] = E * r
            Ub = [sb(U, t) for t in range(8)]
            Eb = [sb(E, t) for t in range(8)]
            for v in range(g + 1, 16):
                xs = [lb(S[b][v], 8 * g + t) for t in range(8)]
                ms = []
                for t in range(8):
                    x = xs[t]
                    for s in range(t):
                        x = x - ms[s] * ust[s][t]
                    ms.append(x * rinvs[t])
                sv, iv = S[b][v], I[b][v]
                for t in range(8):
                    sv = sv - ms[t] * Ub[t]
                    iv = iv - ms[t] * Eb[t]
                S[b][v], I[b][v] = sv, iv
    return out


range_length = 409.6
nugget = 0.5
shift_ratio = 0.01


def matern_block(r, c):
    dx = r[:, 0:1] - c[0:1, :]
    dy = r[:, 1:2] - c[1:2, :]
    d = dx * dx + dy * dy
    return jnp.exp2(d * lax.rsqrt(jnp.maximum(d, 1.0)) * (-math.log2(math.e) / range_length))


def factor_pair(s_refs, o, split, m_ref, l_ref, w_ref, filler=None):
    h = 128
    nb = len(s_refs)

    def part(t, _):
        p = pl.multiple_of(o + h * t, h)
        mats = [[s[pl.ds(pl.multiple_of(p + 8 * v, 8), 8), pl.ds(p, h)] for v in range(16)] for s in s_refs]
        ms = factor_block(mats, None if filler is None else functools.partial(filler, t))
        for b in range(nb):
            for v in range(16):
                m_ref[b, t, 8 * v:8 * v + 8, :] = ms[b][v]

        @pl.when(t == 0)
        def _():
            for b in range(nb):
                s = s_refs[b]
                p1 = pl.multiple_of(o + h, h)
                low = mul_pieces(split(s[pl.ds(p1, h), pl.ds(o, h)]), split(m_ref[b, 0]), dot_nt, 1)
                l_ref[b] = low
                lp = split(low)
                s[pl.ds(p1, h), pl.ds(p1, h)] -= mul_pieces(lp, lp, dot_nt, 1)

        return 0

    lax.fori_loop(0, 2, part, 0)
    for b in range(nb):
        low = mul_pieces(split(l_ref[b]), split(m_ref[b, 0]), dot_nn, 0)
        low = mul_pieces(split(m_ref[b, 1]), split(low), dot_nn, 0)
        w_ref[b, 0:h, 0:h] = m_ref[b, 0]
        w_ref[b, 0:h, h:2 * h] = jnp.zeros((h, h), F32)
        w_ref[b, h:2 * h, 0:h] = -low
        w_ref[b, h:2 * h, h:2 * h] = m_ref[b, 1]


def cov_kernel(pr_ref, pc_ref, hi_out, lo_out, s_ref, x_ref, m_ref, l_ref, w_ref, lh_ref, ll_ref, xh_ref, xl_ref, oh_ref, ol_ref, sems):
    n = s_ref.shape[0]
    ch, bw = 512, 256
    nc = n // ch
    c = pc_ref[...]

    for r in range(nc):
        e = (r + 1) * ch

        def build(k, _):
            o = pl.multiple_of(r * ch + k * 128, 128)
            rows = lax.broadcasted_iota(jnp.int32, (128, e), 0) + o
            cols = lax.broadcasted_iota(jnp.int32, (128, e), 1)
            eye = jnp.where(rows == cols, 1.0, 0.0)
            p = pr_ref[pl.ds(o, 128), :]
            s_ref[pl.ds(o, 128), 0:e] = matern_block(p, c[:, 0:e]) + nugget * eye
            x_ref[pl.ds(o, 128), 0:e] = eye
            return 0

        lax.fori_loop(0, ch // 128, build, 0)
    lh_ref[...] = jnp.zeros((n, bw), BF)
    ll_ref[...] = jnp.zeros((n, bw), BF)
    xh_ref[...] = jnp.zeros((bw, n), BF)
    xl_ref[...] = jnp.zeros((bw, n), BF)
    work = [(r, q, kind) for r in range(nc) for q in range(r + 1) for kind in range(2)]

    def copies(k, e):
        o = pl.multiple_of(k * bw, bw)
        return [
            pltpu.make_async_copy(v.at[pl.ds(o, bw), 0:e], out.at[pl.ds(o, bw), 0:e], sems.at[i, k])
            for i, (v, out) in enumerate(((oh_ref, hi_out), (ol_ref, lo_out)))
        ]

    def step(k, _):
        o = pl.multiple_of(k * bw, bw)

        for r in range(nc):
            @pl.when((k > 0) & (k < 2 * (r + 1)))
            def _():
                rows = slice(r * ch, (r + 1) * ch)
                mine = (lh_ref[pl.ds(o, bw), :], ll_ref[pl.ds(o, bw), :])
                s_ref[rows, pl.ds(o, bw)] -= mul_pieces((lh_ref[rows, :], ll_ref[rows, :]), mine, dot_nt, 1)

        def filler(t, g):
            if g >= len(work):
                return
            r, q, kind = work[g]
            at = pl.multiple_of(r * ch + t * bw, bw)
            cols = slice(q * ch, (q + 1) * ch)
            lr = (lh_ref[pl.ds(at, bw), :], ll_ref[pl.ds(at, bw), :])
            if kind == 0:
                later = lax.broadcasted_iota(jnp.int32, (ch, bw), 0) + q * ch >= o + bw
                lq = tuple(jnp.where(later, w[cols, :], jnp.zeros((), BF)) for w in (lh_ref, ll_ref))
                s_ref[pl.ds(at, bw), cols] -= mul_pieces(lr, lq, dot_nt, 1)
            else:
                x_ref[pl.ds(at, bw), cols] -= mul_pieces(lr, (xh_ref[:, cols], xl_ref[:, cols]), dot_nn, 0)

        factor_pair([s_ref], o, split2, m_ref, l_ref, w_ref, filler)
        M = split2(w_ref[0])
        for r in range(nc):
            e = (r + 1) * ch

            @pl.when(k // 2 == r)
            def _():
                x_hi, x_lo = split2(mul_pieces(M, split2(x_ref[pl.ds(o, bw), 0:e]), dot_nn, 0))
                xh_ref[:, 0:e] = x_hi
                xl_ref[:, 0:e] = x_lo
                oh_ref[pl.ds(o, bw), 0:e] = x_hi
                ol_ref[pl.ds(o, bw), 0:e] = x_lo
                for copy in copies(k, e):
                    copy.start()

            @pl.when(k + 1 < 2 * (r + 1))
            def _():
                rows = slice(r * ch, e)
                lp = mul_pieces(split2(s_ref[rows, pl.ds(o, bw)]), M, dot_nt, 1)
                ids = lax.broadcasted_iota(jnp.int32, (ch, bw), 0) + r * ch
                l_hi, l_lo = split2(jnp.where(ids >= o + bw, lp, 0.0))
                lh_ref[rows, :] = l_hi
                ll_ref[rows, :] = l_lo

            @pl.when(k + 1 == 2 * (r + 1))
            def _():
                lh_ref[r * ch:e, :] = jnp.zeros((ch, bw), BF)
                ll_ref[r * ch:e, :] = jnp.zeros((ch, bw), BF)

        return 0

    lax.fori_loop(0, n // bw, step, 0)
    for k in range(n // bw):
        for copy in copies(k, (k // 2 + 1) * ch):
            copy.wait()


def padded_points(coords):
    return jnp.pad(coords.astype(F32), ((0, 6), (0, 0)))


def cov_factor_inverse(coords):
    n = coords.shape[1]
    pc = padded_points(coords)
    pr = pc.T
    return pl.pallas_call(
        cov_kernel,
        out_shape=(jax.ShapeDtypeStruct((n, n), BF),) * 2,
        scratch_shapes=[
            pltpu.VMEM((n, n), F32),
            pltpu.VMEM((n, n), F32),
            pltpu.VMEM((1, 2, 128, 128), F32),
            pltpu.VMEM((1, 128, 128), F32),
            pltpu.VMEM((1, 256, 256), F32),
            pltpu.VMEM((n, 256), BF),
            pltpu.VMEM((n, 256), BF),
            pltpu.VMEM((256, n), BF),
            pltpu.VMEM((256, n), BF),
            pltpu.VMEM((n, n), BF),
            pltpu.VMEM((n, n), BF),
            pltpu.SemaphoreType.DMA((2, n // 256)),
        ],
        out_specs=(pl.BlockSpec(memory_space=pl.ANY),) * 2,
        compiler_params=pltpu.CompilerParams(vmem_limit_bytes=56 << 20),
        name="cov_factor",
    )(pr, pc)


def gram_factor(s_ref, x_ref, m_ref, l_ref, w_ref, t_ref):
    h = 256

    def part(t, _):
        o = pl.multiple_of(h * t, h)
        factor_pair([s_ref], o, split3, m_ref, l_ref, w_ref)
        x_ref[pl.ds(o, h), pl.ds(o, h)] = w_ref[0]

        @pl.when(t == 0)
        def _():
            low = mul_pieces(split3(s_ref[h:2 * h, 0:h]), split3(w_ref[0]), dot_nt, 1)
            t_ref[...] = low
            lp = split3(low)
            s_ref[h:2 * h, h:2 * h] -= mul_pieces(lp, lp, dot_nt, 1)

        return 0

    lax.fori_loop(0, 2, part, 0)
    low = mul_pieces(split3(t_ref[...]), split3(x_ref[0:h, 0:h]), dot_nn, 0)
    low = mul_pieces(split3(w_ref[0]), split3(low), dot_nn, 0)
    x_ref[h:2 * h, 0:h] = -low
    x_ref[0:h, h:2 * h] = jnp.zeros((h, h), F32)


def tile_kernel(last, *refs):
    if last:
        info_ref, hi_in, lo_in, g_ref, pc_ref, ci_ref, upd_ref = refs[:7]
        refs = refs[7:]
    else:
        info_ref, hi_in, lo_in, g_ref, pc_ref, left_ref, cf_ref = refs[:7]
        refs = refs[7:]
    v_ref, xy_ref, vt_ref, wh_ref, wl_ref, bh_ref, bl_ref, smp_ref, s_ref, x_ref, m_ref, l_ref, w_ref, t_ref, pl_ref = refs[:15]
    hi_ref, lo_ref, sems = refs[15:18]
    if last:
        cf_ref = refs[18]
    n = hi_in.shape[0]
    r = vt_ref.shape[0]
    pieces = g_ref.shape[0]
    local = n // pieces
    blocks = r // 128
    ch, half = 512, 256
    pc = pc_ref[...]
    rank = info_ref[0]
    mask = lax.broadcasted_iota(jnp.int32, (1, r), 1) < rank

    loads = [
        pltpu.make_async_copy(src.at[q * ch:(q + 1) * ch, 0:(q + 1) * ch], dst.at[q * ch:(q + 1) * ch, 0:(q + 1) * ch], sems.at[i, q])
        for q in range(n // ch)
        for i, (src, dst) in enumerate(((hi_in, hi_ref), (lo_in, lo_ref)))
    ]
    for load in loads:
        load.start()

    def place(c, _):
        o = pl.multiple_of(c * local, 32)
        for q in range(blocks):
            v_ref[pl.ds(o, local), q * 128:(q + 1) * 128] = g_ref[c, q * local:(q + 1) * local, :]
        d = g_ref[c, blocks * local:blocks * local + 16, :].astype(F32)
        xy_ref[pl.ds(o, local), 0:16] = d.T[0:local, :]
        return 0

    lax.fori_loop(0, pieces, place, 0)

    def turn(k, _):
        o = pl.multiple_of(k * half, half)
        v = jnp.where(mask, v_ref[pl.ds(o, half), :].astype(F32), 0.0)
        vt_ref[:, pl.ds(o, half)] = v.astype(BF).T
        return 0

    lax.fori_loop(0, n // half, turn, 0)
    for load in loads:
        load.wait()
    for q in range(n // ch):
        o = q * ch
        vt = vt_ref[:, o:]
        w_hi, w_lo = split2(dot_nn(vt, hi_ref[o:, o:o + ch]) + dot_nn(vt, lo_ref[o:, o:o + ch]))
        wh_ref[:, o:o + ch] = w_hi
        wl_ref[:, o:o + ch] = w_lo
    s_ref[...] = jnp.zeros((r, r), F32)
    x_ref[...] = jnp.zeros((r, r), F32)

    def draw(k, _):
        o = pl.multiple_of(k * ch, ch)
        for h in range(ch // half):
            p = pl.multiple_of(o + h * half, half)
            xy = xy_ref[pl.ds(p, half), :]
            xy = jnp.concatenate([xy[:, 0:1] * 256.0 + xy[:, 1:2], xy[:, 2:3] * 256.0 + xy[:, 3:4]], 1)
            b_hi, b_lo = split2(matern_block(xy, pc))
            bh_ref[pl.ds(p, half), :] = b_hi
            bl_ref[pl.ds(p, half), :] = b_lo
        b_hi = bh_ref[pl.ds(o, ch), :]
        wh = wh_ref[...]
        smp = dot_nt(b_hi, wl_ref[...]) + dot_nt(bl_ref[pl.ds(o, ch), :], wh) + dot_nt(b_hi, wh)
        smp_ref[pl.ds(o, ch), :] = smp
        p_h, p_m, p_l = split3(smp)
        t_h = p_h.T
        t_m = p_m.T
        s_ref[...] += dot_nn(t_h, p_h) + dot_nn(t_m, p_m)
        x_ref[...] += dot_nn(t_h, p_m) + dot_nn(t_h, p_l)
        return 0

    lax.fori_loop(0, n // ch, draw, 0)
    cross = x_ref[...]
    gram = s_ref[...] + (cross + cross.T)
    gcol = lax.broadcasted_iota(jnp.int32, (r, r), 1)
    eye = lax.broadcasted_iota(jnp.int32, (r, r), 0) == gcol
    shift = shift_ratio * jnp.sum(jnp.where(eye, gram, 0.0)) / rank.astype(F32)
    s_ref[...] = gram + jnp.where(eye, jnp.where(gcol < rank, shift, 1.0), 0.0)

    gram_factor(s_ref, x_ref, m_ref, l_ref, w_ref, t_ref)

    inv_a = split3(x_ref[0:half, 0:half])
    inv_b = split3(x_ref[half:2 * half, :])

    def base(k, _):
        o = pl.multiple_of(k * ch, ch)
        sp = split3(smp_ref[pl.ds(o, ch), :])
        part_a = mul_pieces(tuple(q[:, 0:half] for q in sp), inv_a, dot_nt, 1)
        part = jnp.concatenate([part_a, mul_pieces(sp, inv_b, dot_nt, 1)], 1).astype(BF)
        pl_ref[pl.ds(o, ch), :] = part
        vt_ref[:, pl.ds(o, ch)] = part.T
        return 0

    lax.fori_loop(0, n // ch, base, 0)
    lt = vt_ref[...]
    for q in range(n // ch):
        o = q * ch
        p_hi, p_lo = split2(dot_nn(lt, bh_ref[:, o:o + ch]) + dot_nn(lt, bl_ref[:, o:o + ch]))
        wh_ref[:, o:o + ch] = p_hi
        wl_ref[:, o:o + ch] = p_lo
    for q in range(n // ch):
        o, e = q * ch, (q + 1) * ch
        ih = hi_ref[o:e, :e]
        ph = wh_ref[:, :e]
        c = dot_nt(ih, wl_ref[:, :e]) + dot_nt(lo_ref[o:e, :e], ph) + dot_nt(ih, ph)
        cf_ref[o:e, :] = c.astype(BF)

    if not last:
        left_ref[...] = pl_ref[pl.ds(pl.multiple_of(info_ref[1] * local, 32), local), :]
        return
    core = jnp.zeros((r, r), F32)
    for q in range(n // ch):
        ct = ci_ref[q * ch:(q + 1) * ch, :].T
        core = core + dot_nn(ct, cf_ref[q * ch:(q + 1) * ch, :])
    core = core.astype(BF)
    for q in range(n // ch):
        upd_ref[q * ch:(q + 1) * ch, :] = dot_nt(pl_ref[q * ch:(q + 1) * ch, :], core).astype(BF)


def tile(last, info, inv_hi, inv_lo, gathered, pc, *other):
    n = inv_hi.shape[0]
    local = n // gathered.shape[0]
    r = (gathered.shape[1] - 16) // local * 128
    vmem = pl.BlockSpec(memory_space=pltpu.VMEM)
    whole = jax.ShapeDtypeStruct((n, r), BF)
    scratch = [
        pltpu.VMEM((n, r), BF),
        pltpu.VMEM((n, 128), F32),
        pltpu.VMEM((r, n), BF),
        pltpu.VMEM((r, n), BF),
        pltpu.VMEM((r, n), BF),
        pltpu.VMEM((n, n), BF),
        pltpu.VMEM((n, n), BF),
        pltpu.VMEM((n, r), F32),
        pltpu.VMEM((r, r), F32),
        pltpu.VMEM((r, r), F32),
        pltpu.VMEM((1, 2, 128, 128), F32),
        pltpu.VMEM((1, 128, 128), F32),
        pltpu.VMEM((1, 256, 256), F32),
        pltpu.VMEM((256, 256), F32),
        pltpu.VMEM((n, r), BF),
        pltpu.VMEM((n, n), BF),
        pltpu.VMEM((n, n), BF),
        pltpu.SemaphoreType.DMA((2, n // 512)),
    ]
    return pl.pallas_call(
        functools.partial(tile_kernel, last),
        in_specs=[pl.BlockSpec(memory_space=pltpu.SMEM)] + [pl.BlockSpec(memory_space=pl.ANY)] * 2 + [vmem] * (2 + len(other)),
        out_specs=vmem if last else (vmem, vmem),
        out_shape=whole if last else (jax.ShapeDtypeStruct((local, r), BF), whole),
        scratch_shapes=scratch + ([pltpu.VMEM((n, r), BF)] if last else []),
        compiler_params=pltpu.CompilerParams(vmem_limit_bytes=56 << 20),
        name="column_tile" if last else "row_tile",
    )(info, inv_hi, inv_lo, gathered, pc, *other)


def shards(diag_coords, panel_coords, test_matrix, ranks):
    n_row = lax.axis_size("row")
    n_col = lax.axis_size("col")
    row_index = lax.axis_index("row")
    col_index = lax.axis_index("col")
    local = panel_coords.shape[2]
    blocks = test_matrix.shape[2] // 128
    digits = jnp.stack([panel_coords[:, 0] >> 8, panel_coords[:, 0] & 255], 1).reshape(4, local).astype(BF)
    digits = jnp.pad(digits, ((0, 12), (0, 128 - local)))
    parts = [test_matrix[0, :, q * 128:(q + 1) * 128] for q in range(blocks)]
    piece = jnp.concatenate(parts + [digits], 0)[None]
    swap = [(r * n_col + c, c * n_col + r) for r in range(n_row) for c in range(n_col)]
    own = lax.all_gather(piece, "col", axis=0, tiled=True)
    turned = lax.all_gather(lax.ppermute(piece, ("row", "col"), swap), "row", axis=0, tiled=True)
    inv_hi, inv_lo = cov_factor_inverse(diag_coords)
    points = padded_points(diag_coords)
    left, coeff = tile(False, jnp.stack([ranks[row_index], col_index]), inv_hi, inv_lo, own, points)
    update = tile(True, jnp.stack([ranks[col_index], col_index]), inv_hi, inv_lo, turned, points, coeff)
    return (left[None], update[None, None])


def solution(mesh):
    in_specs = (P(), P(None, "row", "col"), P("row", "col", None), P())
    out_specs = (P("row", "col", None), P("row", "col", None, None))
    return jax.shard_map(shards, mesh=mesh, in_specs=in_specs, out_specs=out_specs, check_vma=False)
```

```python
import functools
import math

import jax
import jax.numpy as jnp
from jax import lax
from jax.experimental import pallas as pl
from jax.experimental.pallas import tpu as pltpu
from jax.sharding import PartitionSpec as P

F32 = jnp.float32
BF = jnp.bfloat16


def split2(a):
    hi = a.astype(BF)
    lo = (a - hi.astype(F32)).astype(BF)
    return hi, lo


def split3(a):
    hi = a.astype(BF)
    r = a - hi.astype(F32)
    mid = r.astype(BF)
    return hi, mid, (r - mid.astype(F32)).astype(BF)


def dot_nn(a, b):
    return lax.dot_general(a, b, (((1,), (0,)), ((), ())), preferred_element_type=F32)


def dot_nt(a, b):
    return lax.dot_general(a, b, (((1,), (1,)), ((), ())), preferred_element_type=F32)


def mul_pieces(a, b, dot, axis_b):
    if len(a) == 2:
        ah, al = a
        bh, bl = b
        return dot(jnp.concatenate([ah, al], 1), jnp.concatenate([bh, bh], axis_b)) + dot(ah, bl)
    ah, am, al = a
    bh, bm, bl = b
    hm = jnp.concatenate([ah, am], 1)
    out = dot(jnp.concatenate([ah, al], 1), jnp.concatenate([bl, bh], axis_b))
    out = out + dot(hm, jnp.concatenate([bm, bm], axis_b))
    return out + dot(hm, jnp.concatenate([bh, bh], axis_b))


def factor_block(mats, filler=None):
    sub = lax.broadcasted_iota(jnp.int32, (8, 128), 0)
    lane = lax.broadcasted_iota(jnp.int32, (8, 128), 1)

    def sb(a, p):
        return jnp.broadcast_to(a[p:p + 1, :], (8, 128))

    def lb(a, c):
        return jnp.broadcast_to(a[:, c:c + 1], (8, 128))

    nb = len(mats)
    S = [list(m) for m in mats]
    I = [[jnp.where(lane == sub + 8 * v, 1.0, 0.0).astype(F32) for v in range(16)] for _ in mats]
    out = [[None] * 16 for _ in mats]
    for g in range(16):
        if filler is not None:
            filler(g)
        st = []
        for b in range(nb):
            U, E = S[b][g], I[b][g]
            C = [lb(U, 8 * g + t) for t in range(8)]
            st.append([U, E, C, [], [], []])
        for p in range(0, 8, 2):
            for b in range(nb):
                U, E, C, rinvs, ust, ds = st[b]
                first, second = sb(C[p], p), sb(C[p + 1], p + 1)
                rows = {t: sb(C[t], p) for t in range(p + 1, 8)}
                det = first * second - rows[p + 1] * rows[p + 1]
                r0 = 1.0 / first
                r1 = first * (1.0 / det)
                m0 = jnp.where(sub > p, C[p] * r0, 0.0)
                m1 = jnp.where(sub > p + 1, (C[p + 1] - m0 * rows[p + 1]) * r1, 0.0)
                ratio = rows[p + 1] * r0
                later = {t: sb(C[t], p + 1) - ratio * rows[t] for t in range(p + 2, 8)}
                for t in range(p + 2, 8):
                    C[t] = C[t] - m0 * rows[t] - m1 * later[t]
                U = U - m0 * sb(U, p)
                E = E - m0 * sb(E, p)
                st[b][0] = U - m1 * sb(U, p + 1)
                st[b][1] = E - m1 * sb(E, p + 1)
                rinvs += [r0, r1]
                ust += [rows, later]
                ds += [first, det * r0]
        for b in range(nb):
            U, E, C, rinvs, ust, ds = st[b]
            dv = ds[0]
            for p in range(1, 8):
                dv = jnp.where(sub == p, ds[p], dv)
            r = lax.rsqrt(dv)
            r = r * (1.5 - 0.5 * dv * r * r)
            out[b][g] = E * r
            Ub = [sb(U, t) for t in range(8)]
            Eb = [sb(E, t) for t in range(8)]
            for v in range(g + 1, 16):
                xs = [lb(S[b][v], 8 * g + t) for t in range(8)]
                ms = []
                for t in range(8):
                    x = xs[t]
                    for s in range(t):
                        x = x - ms[s] * ust[s][t]
                    ms.append(x * rinvs[t])
                sv, iv = S[b][v], I[b][v]
                for t in range(8):
                    sv = sv - ms[t] * Ub[t]
                    iv = iv - ms[t] * Eb[t]
                S[b][v], I[b][v] = sv, iv
    return out


range_length = 409.6
nugget = 0.5
shift_ratio = 0.01


def matern_block(r, c):
    dx = r[:, 0:1] - c[0:1, :]
    dy = r[:, 1:2] - c[1:2, :]
    d = dx * dx + dy * dy
    return jnp.exp2(d * lax.rsqrt(jnp.maximum(d, 1.0)) * (-math.log2(math.e) / range_length))


def factor_pair(s_refs, o, split, m_ref, l_ref, w_ref, filler=None):
    h = 128
    nb = len(s_refs)

    def part(t, _):
        p = pl.multiple_of(o + h * t, h)
        mats = [[s[pl.ds(pl.multiple_of(p + 8 * v, 8), 8), pl.ds(p, h)] for v in range(16)] for s in s_refs]
        ms = factor_block(mats, None if filler is None else functools.partial(filler, t))
        for b in range(nb):
            for v in range(16):
                m_ref[b, t, 8 * v:8 * v + 8, :] = ms[b][v]

        @pl.when(t == 0)
        def _():
            for b in range(nb):
                s = s_refs[b]
                p1 = pl.multiple_of(o + h, h)
                low = mul_pieces(split(s[pl.ds(p1, h), pl.ds(o, h)]), split(m_ref[b, 0]), dot_nt, 1)
                l_ref[b] = low
                lp = split(low)
                s[pl.ds(p1, h), pl.ds(p1, h)] -= mul_pieces(lp, lp, dot_nt, 1)

        return 0

    lax.fori_loop(0, 2, part, 0)
    for b in range(nb):
        low = mul_pieces(split(l_ref[b]), split(m_ref[b, 0]), dot_nn, 0)
        low = mul_pieces(split(m_ref[b, 1]), split(low), dot_nn, 0)
        w_ref[b, 0:h, 0:h] = m_ref[b, 0]
        w_ref[b, 0:h, h:2 * h] = jnp.zeros((h, h), F32)
        w_ref[b, h:2 * h, 0:h] = -low
        w_ref[b, h:2 * h, h:2 * h] = m_ref[b, 1]


def cov_kernel(pr_ref, pc_ref, hi_out, lo_out, s_ref, x_ref, m_ref, l_ref, w_ref, lh_ref, ll_ref, xh_ref, xl_ref, oh_ref, ol_ref, sems):
    n = s_ref.shape[0]
    ch, bw = 512, 256
    nc = n // ch
    c = pc_ref[...]

    for r in range(nc):
        e = (r + 1) * ch

        def build(k, _):
            o = pl.multiple_of(r * ch + k * 128, 128)
            rows = lax.broadcasted_iota(jnp.int32, (128, e), 0) + o
            cols = lax.broadcasted_iota(jnp.int32, (128, e), 1)
            eye = jnp.where(rows == cols, 1.0, 0.0)
            p = pr_ref[pl.ds(o, 128), :]
            s_ref[pl.ds(o, 128), 0:e] = matern_block(p, c[:, 0:e]) + nugget * eye
            x_ref[pl.ds(o, 128), 0:e] = eye
            return 0

        lax.fori_loop(0, ch // 128, build, 0)
    lh_ref[...] = jnp.zeros((n, bw), BF)
    ll_ref[...] = jnp.zeros((n, bw), BF)
    xh_ref[...] = jnp.zeros((bw, n), BF)
    xl_ref[...] = jnp.zeros((bw, n), BF)
    work = [(r, q, kind) for r in range(nc) for q in range(r + 1) for kind in range(2)]

    def copies(k, e):
        o = pl.multiple_of(k * bw, bw)
        return [
            pltpu.make_async_copy(v.at[pl.ds(o, bw), 0:e], out.at[pl.ds(o, bw), 0:e], sems.at[i, k])
            for i, (v, out) in enumerate(((oh_ref, hi_out), (ol_ref, lo_out)))
        ]

    def step(k, _):
        o = pl.multiple_of(k * bw, bw)

        for r in range(nc):
            @pl.when((k > 0) & (k < 2 * (r + 1)))
            def _():
                rows = slice(r * ch, (r + 1) * ch)
                mine = (lh_ref[pl.ds(o, bw), :], ll_ref[pl.ds(o, bw), :])
                s_ref[rows, pl.ds(o, bw)] -= mul_pieces((lh_ref[rows, :], ll_ref[rows, :]), mine, dot_nt, 1)

        def filler(t, g):
            if g >= len(work):
                return
            r, q, kind = work[g]
            at = pl.multiple_of(r * ch + t * bw, bw)
            cols = slice(q * ch, (q + 1) * ch)
            lr = (lh_ref[pl.ds(at, bw), :], ll_ref[pl.ds(at, bw), :])
            if kind == 0:
                later = lax.broadcasted_iota(jnp.int32, (ch, bw), 0) + q * ch >= o + bw
                lq = tuple(jnp.where(later, w[cols, :], jnp.zeros((), BF)) for w in (lh_ref, ll_ref))
                s_ref[pl.ds(at, bw), cols] -= mul_pieces(lr, lq, dot_nt, 1)
            else:
                x_ref[pl.ds(at, bw), cols] -= mul_pieces(lr, (xh_ref[:, cols], xl_ref[:, cols]), dot_nn, 0)

        factor_pair([s_ref], o, split2, m_ref, l_ref, w_ref, filler)
        M = split2(w_ref[0])
        for r in range(nc):
            e = (r + 1) * ch

            @pl.when(k // 2 == r)
            def _():
                x_hi, x_lo = split2(mul_pieces(M, split2(x_ref[pl.ds(o, bw), 0:e]), dot_nn, 0))
                xh_ref[:, 0:e] = x_hi
                xl_ref[:, 0:e] = x_lo
                oh_ref[pl.ds(o, bw), 0:e] = x_hi
                ol_ref[pl.ds(o, bw), 0:e] = x_lo
                for copy in copies(k, e):
                    copy.start()

            @pl.when(k + 1 < 2 * (r + 1))
            def _():
                rows = slice(r * ch, e)
                lp = mul_pieces(split2(s_ref[rows, pl.ds(o, bw)]), M, dot_nt, 1)
                ids = lax.broadcasted_iota(jnp.int32, (ch, bw), 0) + r * ch
                l_hi, l_lo = split2(jnp.where(ids >= o + bw, lp, 0.0))
                lh_ref[rows, :] = l_hi
                ll_ref[rows, :] = l_lo

            @pl.when(k + 1 == 2 * (r + 1))
            def _():
                lh_ref[r * ch:e, :] = jnp.zeros((ch, bw), BF)
                ll_ref[r * ch:e, :] = jnp.zeros((ch, bw), BF)

        return 0

    lax.fori_loop(0, n // bw, step, 0)
    for k in range(n // bw):
        for copy in copies(k, (k // 2 + 1) * ch):
            copy.wait()


def padded_points(coords):
    return jnp.pad(coords.astype(F32), ((0, 6), (0, 0)))


def cov_factor_inverse(coords):
    n = coords.shape[1]
    pc = padded_points(coords)
    pr = pc.T
    return pl.pallas_call(
        cov_kernel,
        out_shape=(jax.ShapeDtypeStruct((n, n), BF),) * 2,
        scratch_shapes=[
            pltpu.VMEM((n, n), F32),
            pltpu.VMEM((n, n), F32),
            pltpu.VMEM((1, 2, 128, 128), F32),
            pltpu.VMEM((1, 128, 128), F32),
            pltpu.VMEM((1, 256, 256), F32),
            pltpu.VMEM((n, 256), BF),
            pltpu.VMEM((n, 256), BF),
            pltpu.VMEM((256, n), BF),
            pltpu.VMEM((256, n), BF),
            pltpu.VMEM((n, n), BF),
            pltpu.VMEM((n, n), BF),
            pltpu.SemaphoreType.DMA((2, n // 256)),
        ],
        out_specs=(pl.BlockSpec(memory_space=pl.ANY),) * 2,
        compiler_params=pltpu.CompilerParams(vmem_limit_bytes=56 << 20),
        name="cov_factor",
    )(pr, pc)


def gram_factor(s_ref, x_ref, m_ref, l_ref, w_ref, t_ref):
    h = 256

    def part(t, _):
        o = pl.multiple_of(h * t, h)
        factor_pair([s_ref], o, split3, m_ref, l_ref, w_ref)
        x_ref[pl.ds(o, h), pl.ds(o, h)] = w_ref[0]

        @pl.when(t == 0)
        def _():
            low = mul_pieces(split3(s_ref[h:2 * h, 0:h]), split3(w_ref[0]), dot_nt, 1)
            t_ref[...] = low
            lp = split3(low)
            s_ref[h:2 * h, h:2 * h] -= mul_pieces(lp, lp, dot_nt, 1)

        return 0

    lax.fori_loop(0, 2, part, 0)
    low = mul_pieces(split3(t_ref[...]), split3(x_ref[0:h, 0:h]), dot_nn, 0)
    low = mul_pieces(split3(w_ref[0]), split3(low), dot_nn, 0)
    x_ref[h:2 * h, 0:h] = -low
    x_ref[0:h, h:2 * h] = jnp.zeros((h, h), F32)


def tile_kernel(last, *refs):
    if last:
        info_ref, hi_in, lo_in, g_ref, pc_ref, ci_ref, upd_ref = refs[:7]
        refs = refs[7:]
    else:
        info_ref, hi_in, lo_in, g_ref, pc_ref, left_ref, cf_ref = refs[:7]
        refs = refs[7:]
    v_ref, xy_ref, vt_ref, wh_ref, wl_ref, bh_ref, bl_ref, smp_ref, s_ref, x_ref, m_ref, l_ref, w_ref, t_ref, pl_ref = refs[:15]
    hi_ref, lo_ref, sems = refs[15:18]
    if last:
        cf_ref = refs[18]
    n = hi_in.shape[0]
    r = vt_ref.shape[0]
    pieces = g_ref.shape[0]
    local = n // pieces
    blocks = r // 128
    ch, half = 512, 256
    pc = pc_ref[...]
    rank = info_ref[0]
    mask = lax.broadcasted_iota(jnp.int32, (1, r), 1) < rank

    loads = [
        pltpu.make_async_copy(src.at[q * ch:(q + 1) * ch, 0:(q + 1) * ch], dst.at[q * ch:(q + 1) * ch, 0:(q + 1) * ch], sems.at[i, q])
        for q in range(n // ch)
        for i, (src, dst) in enumerate(((hi_in, hi_ref), (lo_in, lo_ref)))
    ]
    for load in loads:
        load.start()

    def place(c, _):
        o = pl.multiple_of(c * local, 32)
        for q in range(blocks):
            v_ref[pl.ds(o, local), q * 128:(q + 1) * 128] = g_ref[c, q * local:(q + 1) * local, :]
        d = g_ref[c, blocks * local:blocks * local + 16, :].astype(F32)
        xy_ref[pl.ds(o, local), 0:16] = d.T[0:local, :]
        return 0

    lax.fori_loop(0, pieces, place, 0)

    def turn(k, _):
        o = pl.multiple_of(k * half, half)
        v = jnp.where(mask, v_ref[pl.ds(o, half), :].astype(F32), 0.0)
        vt_ref[:, pl.ds(o, half)] = v.astype(BF).T
        return 0

    lax.fori_loop(0, n // half, turn, 0)

    def build(k, _):
        o = pl.multiple_of(k * half, half)
        xy = xy_ref[pl.ds(o, half), :]
        xy = jnp.concatenate([xy[:, 0:1] * 256.0 + xy[:, 1:2], xy[:, 2:3] * 256.0 + xy[:, 3:4]], 1)
        b_hi, b_lo = split2(matern_block(xy, pc))
        bh_ref[pl.ds(o, half), :] = b_hi
        bl_ref[pl.ds(o, half), :] = b_lo
        return 0

    lax.fori_loop(0, n // half, build, 0)
    for load in loads:
        load.wait()
    for q in range(n // ch):
        o = q * ch
        vt = vt_ref[:, o:]
        w_hi, w_lo = split2(dot_nn(vt, hi_ref[o:, o:o + ch]) + dot_nn(vt, lo_ref[o:, o:o + ch]))
        wh_ref[:, o:o + ch] = w_hi
        wl_ref[:, o:o + ch] = w_lo
    s_ref[...] = jnp.zeros((r, r), F32)
    x_ref[...] = jnp.zeros((r, r), F32)

    def draw(k, _):
        o = pl.multiple_of(k * ch, ch)
        b_hi = bh_ref[pl.ds(o, ch), :]
        wh = wh_ref[...]
        smp = dot_nt(b_hi, wl_ref[...]) + dot_nt(bl_ref[pl.ds(o, ch), :], wh) + dot_nt(b_hi, wh)
        smp_ref[pl.ds(o, ch), :] = smp
        p_h, p_m, p_l = split3(smp)
        t_h = p_h.T
        t_m = p_m.T
        s_ref[...] += dot_nn(t_h, p_h) + dot_nn(t_m, p_m)
        x_ref[...] += dot_nn(t_h, p_m) + dot_nn(t_h, p_l)
        return 0

    lax.fori_loop(0, n // ch, draw, 0)
    cross = x_ref[...]
    gram = s_ref[...] + (cross + cross.T)
    gcol = lax.broadcasted_iota(jnp.int32, (r, r), 1)
    eye = lax.broadcasted_iota(jnp.int32, (r, r), 0) == gcol
    trace = jnp.full((1, 1), jnp.sum(jnp.where(eye, gram, 0.0)), F32)
    shift = shift_ratio / rank.astype(F32)
    s_ref[...] = gram * (1.0 / trace) + jnp.where(eye, jnp.where(gcol < rank, shift, 1.0), 0.0)
    scale = lax.rsqrt(trace)
    scale = scale * (1.5 - 0.5 * trace * scale * scale)

    gram_factor(s_ref, x_ref, m_ref, l_ref, w_ref, t_ref)

    inv_a = split2(x_ref[0:half, 0:half])
    inv_b = split2(x_ref[half:2 * half, :])

    def base(k, _):
        o = pl.multiple_of(k * ch, ch)
        sp = split2(smp_ref[pl.ds(o, ch), :] * scale)
        part_a = mul_pieces(tuple(q[:, 0:half] for q in sp), inv_a, dot_nt, 1)
        part = jnp.concatenate([part_a, mul_pieces(sp, inv_b, dot_nt, 1)], 1).astype(BF)
        pl_ref[pl.ds(o, ch), :] = part
        vt_ref[:, pl.ds(o, ch)] = part.T
        return 0

    lax.fori_loop(0, n // ch, base, 0)
    lt = vt_ref[...]
    for q in range(n // ch):
        o = q * ch
        p_hi, p_lo = split2(dot_nn(lt, bh_ref[:, o:o + ch]) + dot_nn(lt, bl_ref[:, o:o + ch]))
        wh_ref[:, o:o + ch] = p_hi
        wl_ref[:, o:o + ch] = p_lo
    for q in range(n // ch):
        o, e = q * ch, (q + 1) * ch
        ih = hi_ref[o:e, :e]
        ph = wh_ref[:, :e]
        c = dot_nt(ih, wl_ref[:, :e]) + dot_nt(lo_ref[o:e, :e], ph) + dot_nt(ih, ph)
        cf_ref[o:e, :] = c.astype(BF)

    if not last:
        left_ref[...] = pl_ref[pl.ds(pl.multiple_of(info_ref[1] * local, 32), local), :]
        return
    core = jnp.zeros((r, r), F32)
    for q in range(n // ch):
        ct = ci_ref[q * ch:(q + 1) * ch, :].T
        core = core + dot_nn(ct, cf_ref[q * ch:(q + 1) * ch, :])
    core = core.astype(BF)
    for q in range(n // ch):
        upd_ref[q * ch:(q + 1) * ch, :] = dot_nt(pl_ref[q * ch:(q + 1) * ch, :], core).astype(BF)


def tile(last, info, inv_hi, inv_lo, gathered, pc, *other):
    n = inv_hi.shape[0]
    local = n // gathered.shape[0]
    r = (gathered.shape[1] - 16) // local * 128
    vmem = pl.BlockSpec(memory_space=pltpu.VMEM)
    whole = jax.ShapeDtypeStruct((n, r), BF)
    scratch = [
        pltpu.VMEM((n, r), BF),
        pltpu.VMEM((n, 128), F32),
        pltpu.VMEM((r, n), BF),
        pltpu.VMEM((r, n), BF),
        pltpu.VMEM((r, n), BF),
        pltpu.VMEM((n, n), BF),
        pltpu.VMEM((n, n), BF),
        pltpu.VMEM((n, r), F32),
        pltpu.VMEM((r, r), F32),
        pltpu.VMEM((r, r), F32),
        pltpu.VMEM((1, 2, 128, 128), F32),
        pltpu.VMEM((1, 128, 128), F32),
        pltpu.VMEM((1, 256, 256), F32),
        pltpu.VMEM((256, 256), F32),
        pltpu.VMEM((n, r), BF),
        pltpu.VMEM((n, n), BF),
        pltpu.VMEM((n, n), BF),
        pltpu.SemaphoreType.DMA((2, n // 512)),
    ]
    return pl.pallas_call(
        functools.partial(tile_kernel, last),
        in_specs=[pl.BlockSpec(memory_space=pltpu.SMEM)] + [pl.BlockSpec(memory_space=pl.ANY)] * 2 + [vmem] * (2 + len(other)),
        out_specs=vmem if last else (vmem, vmem),
        out_shape=whole if last else (jax.ShapeDtypeStruct((local, r), BF), whole),
        scratch_shapes=scratch + ([pltpu.VMEM((n, r), BF)] if last else []),
        compiler_params=pltpu.CompilerParams(vmem_limit_bytes=56 << 20),
        name="column_tile" if last else "row_tile",
    )(info, inv_hi, inv_lo, gathered, pc, *other)


def shards(diag_coords, panel_coords, test_matrix, ranks):
    n_row = lax.axis_size("row")
    n_col = lax.axis_size("col")
    row_index = lax.axis_index("row")
    col_index = lax.axis_index("col")
    local = panel_coords.shape[2]
    blocks = test_matrix.shape[2] // 128
    digits = jnp.stack([panel_coords[:, 0] >> 8, panel_coords[:, 0] & 255], 1).reshape(4, local).astype(BF)
    digits = jnp.pad(digits, ((0, 12), (0, 128 - local)))
    parts = [test_matrix[0, :, q * 128:(q + 1) * 128] for q in range(blocks)]
    piece = jnp.concatenate(parts + [digits], 0)[None]
    swap = [(r * n_col + c, c * n_col + r) for r in range(n_row) for c in range(n_col)]
    own = lax.all_gather(piece, "col", axis=0, tiled=True)
    turned = lax.all_gather(lax.ppermute(piece, ("row", "col"), swap), "row", axis=0, tiled=True)
    inv_hi, inv_lo = cov_factor_inverse(diag_coords)
    points = padded_points(diag_coords)
    left, coeff = tile(False, jnp.stack([ranks[row_index], col_index]), inv_hi, inv_lo, own, points)
    update = tile(True, jnp.stack([ranks[col_index], col_index]), inv_hi, inv_lo, turned, points, coeff)
    return (left[None], update[None, None])


def solution(mesh):
    in_specs = (P(), P(None, "row", "col"), P("row", "col", None), P())
    out_specs = (P("row", "col", None), P("row", "col", None, None))
    return jax.shard_map(shards, mesh=mesh, in_specs=in_specs, out_specs=out_specs, check_vma=False)
```
